32 devices in a mesh: geom: 2 (over x), occ: 16 (over z, y, core).
Axes of the slice: x: 2, y: 2, z: 4, core: 2. Of those that a mesh axis runs over, the one named last changes fastest.
Arguments:
- three_index: bfloat16 [32, 512, 2048], P(('geom', 'occ')), parts along dimension 0, may hold values from -0.59765625 to 0.59765625
- occ_energy: float32 [32], P(('geom', 'occ')), parts along dimension 0, may hold values from -1.5 to -0.5
- vir_energy: float32 [1024], P('geom'), parts along dimension 0, may hold values from 0.5 to 3
Outputs:
- aux_density: bfloat16 [32, 512, 2048], P(('geom', 'occ')), parts along dimension 0
- vir_density: float32 [1024, 512], P(('geom', 'occ')), parts along dimension 0
The draws below stay inside these ranges and needn't reach their ends.
There are 2 independent parts, one for each index of `geom`. The reference program is written for one: setup_inputs(seed, part) draws one part's arguments, and reference() takes and returns one part's arrays. A program takes and returns all parts, laid end to end along the dimension named above; each array names one. Nothing has to cross between parts.
All inputs are finite; a program needn't handle non-finite values.
Results may differ from the reference program's by a relative error of at most 0.0055.
Values may be sent and summed in bfloat16 or wider, within the bound.
No kernel may reach another device: no remote copies, remote signals or barrier semaphores. Data moves between devices by JAX's collectives and lax.ppermute only.
A program may use at most 64 MiB of HBM per device.

```python
import jax
import jax.numpy as jnp
from jax import lax

VIR = 512
NAUX = 2048
OCC_DEV = 1
REACH = 2
OCC = 16
N_OCC = 16


def block_scale(stream_key, dims, pieces, smallest, top_value):
    loudness = 1.0
    for position, parts in pieces:
        draws = jax.random.uniform(jax.random.fold_in(jax.random.fold_in(stream_key, 6), position), (parts,), jnp.float32, smallest / len(pieces), top_value / len(pieces))
        loudness = loudness * jnp.repeat(jnp.exp(draws), dims[position] // parts).reshape((-1,) + (1,) * (len(dims) - 1 - position))
    return loudness


def normal_values(own_key, dims, deviation, most, pieces=(), kind=jnp.bfloat16):
    array = deviation * jax.random.normal(own_key, dims, jnp.float32)
    if pieces:
        array = array * block_scale(own_key, dims, pieces, -0.22, 0.18)
    return jnp.clip(array, -most, most).astype(kind)


def setup_inputs(seed: int = 0, part: int = 0) -> dict:
    streams_of = jax.random.split(jax.random.key(seed), 4)
    part_keys = jax.random.split(jax.random.fold_in(streams_of[3], part), 4)
    return {
        "three_index": normal_values(part_keys[0], (OCC, VIR, NAUX), 0.1, 0.59765625, ((0, 16),)),
        "occ_energy": jnp.clip(-1.5 + 1.0 * jax.random.uniform(part_keys[1], (OCC,), jnp.float32) ** block_scale(part_keys[1], (OCC,), ((0, 16),), -0.2, 0.2), -1.5, -0.5),
        "vir_energy": jnp.clip(jax.random.uniform(part_keys[2], (VIR,), jnp.float32, 0.5, 3.0), 0.5, 3.0),
    }


def pair_terms(carry, own, own_eps, other, other_eps, vir_energy):
    density, vir_density = carry
    coulomb = jnp.einsum("iap,jbp->ijab", own.astype(jnp.float32), other.astype(jnp.float32))
    divisor = own_eps[:, None, None, None] + other_eps[None, :, None, None] - vir_energy[None, None, :, None] - vir_energy[None, None, None, :]
    amplitude = coulomb / divisor
    mixed = (2.0 * amplitude - jnp.swapaxes(amplitude, 2, 3)).astype(jnp.bfloat16)
    amp_half = amplitude.astype(jnp.bfloat16)
    density = density + jnp.einsum("ijab,jbp->iap", mixed.astype(jnp.float32), other.astype(jnp.float32))
    vir_density = vir_density + jnp.einsum("ijac,ijbc->ab", amp_half.astype(jnp.float32), mixed.astype(jnp.float32))
    return density, vir_density


def reference(three_index, occ_energy, vir_energy):
    blocks = three_index.reshape(N_OCC, OCC_DEV, VIR, NAUX)
    energies = occ_energy.reshape(N_OCC, OCC_DEV)

    def one_device(owner):
        own = blocks[owner]
        own_eps = energies[owner]
        carry = (jnp.zeros((OCC_DEV, VIR, NAUX), jnp.float32), jnp.zeros((VIR, VIR), jnp.float32))
        for offset in range(-REACH, REACH + 1):
            partner = ((owner + offset) % N_OCC).astype(jnp.int32)
            other = lax.dynamic_index_in_dim(blocks, partner, 0, keepdims=False)
            other_eps = lax.dynamic_index_in_dim(energies, partner, 0, keepdims=False)
            carry = pair_terms(carry, own, own_eps, other, other_eps, vir_energy)
        return carry[0].astype(jnp.bfloat16), carry[1]

    densities, vir_parts = lax.map(one_device, jnp.arange(N_OCC, dtype=jnp.int32))
    aux_density = densities.reshape(OCC, VIR, NAUX)
    vir_density = jnp.sum(vir_parts, axis=0) * (2.0 / (OCC * (2 * REACH + 1)))
    return aux_density, vir_density
```

```python
import functools

import jax
import jax.numpy as jnp
from jax import lax
from jax.experimental import pallas as pl
from jax.experimental.pallas import tpu as pltpu
from jax.sharding import PartitionSpec as P

REACH = 2
CHUNKS = 4

F32 = jnp.float32
BF16 = jnp.bfloat16
NT = (((1,), (1,)), ((), ()))
TN = (((0,), (0,)), ((), ()))
NN = (((1,), (0,)), ((), ()))


def tied(values, token):
    return lax.optimization_barrier((values, token))[0]


def stage_kernel(steps, n_src, has_carry, last, vir, naux, role_ref, eps_ref, own_ref, *rest):
    vir_ref = rest[0]
    rest = rest[1:]
    srcs = rest[:n_src]
    rest = rest[n_src:]
    if has_carry:
        dens_in, vdens_in = rest[:2]
        rest = rest[2:]
    dens_out, vdens_out = rest[:2]
    own, other, amp, half, mixed, acc, vacc, vcol, obf, sems = rest[2:]
    role = role_ref[0]
    rows = 256
    cols = 512

    pltpu.make_async_copy(own_ref, own, sems.at[0]).start()
    if has_carry:
        pltpu.make_async_copy(dens_in, acc, sems.at[1]).start()
        pltpu.make_async_copy(vdens_in, vacc, sems.at[2]).start()

    def fetch(which, sources):
        if sources == "own":
            return
        start = 0
        for s in sources:
            size = srcs[s].shape[0]
            pltpu.make_async_copy(srcs[s], other.at[which % 2, pl.ds(start, size)], sems.at[3 + which % 2]).start()
            start += size

    def fetch_step(n):
        _, by_role, _ = steps[n]
        if by_role[0] == by_role[1]:
            fetch(n, by_role[0])
            return
        for r in (0, 1):
            if by_role[r] is not None:
                @pl.when(role == r)
                def _(r=r):
                    fetch(n, by_role[r])

    fetch_step(0)
    vcol[...] = jnp.transpose(jnp.broadcast_to(vir_ref[...], (128, vir)))
    pltpu.make_async_copy(own_ref, own, sems.at[0]).wait()
    state = {"acc": has_carry, "vacc": has_carry, "waited": not has_carry}

    for n, (slot, by_role, weights) in enumerate(steps):
        if n + 1 < len(steps):
            fetch_step(n + 1)

        def body(n=n, slot=slot, by_role=by_role, weights=weights):
            if by_role[0] == "own":
                oth = own
            else:
                oth = other.at[n % 2]
                pltpu.make_async_copy(own_ref, oth, sems.at[3 + n % 2]).wait()
            eps = eps_ref[0] + eps_ref[slot]
            for a in range(0, vir, rows):
                coulomb = lax.dot_general(own[pl.ds(a, rows), :], oth[...], NT, preferred_element_type=F32)
                col = vcol[pl.ds(a, rows), :]
                divisor = eps - jnp.concatenate([col] * (vir // 128), axis=1) - vir_ref[...]
                value = coulomb / divisor
                amp[pl.ds(a, rows), :] = value
                half[pl.ds(a, rows), :] = value.astype(BF16)
            for a in range(0, vir, rows):
                for b in range(0, vir, rows):
                    x = amp[pl.ds(a, rows), pl.ds(b, rows)]
                    y = amp[pl.ds(b, rows), pl.ds(a, rows)]
                    mixed[pl.ds(a, rows), pl.ds(b, rows)] = (2.0 * x - jnp.transpose(y)).astype(BF16)
            first_v = not state["vacc"]

            def add_v(dims, fresh):
                for a in range(0, vir, rows):
                    if dims is NT:
                        term = lax.dot_general(half[pl.ds(a, rows), :], mixed[...], NT, preferred_element_type=F32)
                    else:
                        term = lax.dot_general(half[:, pl.ds(a, rows)], mixed[...], TN, preferred_element_type=F32)
                    if fresh:
                        vacc[pl.ds(a, rows), :] = term
                    else:
                        vacc[pl.ds(a, rows), :] += term

            if not state["waited"] and n == 0:
                pltpu.make_async_copy(dens_in, acc, sems.at[1]).wait()
                pltpu.make_async_copy(vdens_in, vacc, sems.at[2]).wait()
            for term, dims in ((0, NT), (1, TN)):
                on = [weights[r][term] for r in (0, 1)]
                if on[0] and on[1]:
                    add_v(dims, first_v)
                    first_v = False
                elif on[0] or on[1]:
                    @pl.when(role == (0 if on[0] else 1))
                    def _(dims=dims):
                        add_v(dims, False)
            fresh = not state["acc"]
            final = last and n == len(steps) - 1
            for b in range(0, naux, cols):
                term = lax.dot_general(mixed[...], oth[:, pl.ds(b, cols)], NN, preferred_element_type=F32)
                if not fresh:
                    term = acc[:, pl.ds(b, cols)] + term
                acc[:, pl.ds(b, cols)] = term

        if by_role[0] is None:
            @pl.when(role == 1)
            def _():
                body()
        elif by_role[1] is None:
            @pl.when(role == 0)
            def _():
                body()
        else:
            body()
            state["acc"] = True
            state["vacc"] = True
        if n == 0 and has_carry and (by_role[0] is None or by_role[1] is None):
            @pl.when(role == (0 if by_role[0] is None else 1))
            def _():
                pltpu.make_async_copy(dens_in, acc, sems.at[1]).wait()
                pltpu.make_async_copy(vdens_in, vacc, sems.at[2]).wait()

    if last:
        obf[...] = acc[...].astype(BF16)
        final_copy = pltpu.make_async_copy(obf, dens_out, sems.at[1])
    else:
        final_copy = pltpu.make_async_copy(acc, dens_out, sems.at[1])
    final_copy.start()
    v_copy = pltpu.make_async_copy(vacc, vdens_out, sems.at[2])
    v_copy.start()
    final_copy.wait()
    v_copy.wait()


def stage(name, steps, sources, carry, last, role, eps, own, vir_row):
    vir, naux = own.shape
    hbm = pl.BlockSpec(memory_space=pl.ANY)
    smem = pl.BlockSpec(memory_space=pltpu.SMEM)
    body = functools.partial(stage_kernel, steps, len(sources), carry is not None, last, vir, naux)
    return pl.pallas_call(
        body,
        name=name,
        in_specs=[smem, smem, hbm, pl.BlockSpec(memory_space=pltpu.VMEM)] + [hbm] * (len(sources) + (2 if carry else 0)),
        out_specs=(hbm, hbm),
        out_shape=(
            jax.ShapeDtypeStruct((vir, naux), BF16 if last else F32),
            jax.ShapeDtypeStruct((vir, vir), F32),
        ),
        scratch_shapes=[
            pltpu.VMEM((vir, naux), BF16),
            pltpu.VMEM((2, vir, naux), BF16),
            pltpu.VMEM((vir, vir), F32),
            pltpu.VMEM((vir, vir), BF16),
            pltpu.VMEM((vir, vir), BF16),
            pltpu.VMEM((vir, naux), F32),
            pltpu.VMEM((vir, vir), F32),
            pltpu.VMEM((vir, 128), F32),
            pltpu.VMEM((vir, naux) if last else (16, 128), BF16),
            pltpu.SemaphoreType.DMA((5,)),
        ],
        compiler_params=pltpu.CompilerParams(vmem_limit_bytes=40 << 20),
    )(role, eps, own, vir_row, *sources, *(carry if carry else ()))


def per_device(three_index, occ_energy, vir_energy):
    peers = lax.axis_size("occ")
    own = three_index[0]
    vir, naux = own.shape
    index = lax.axis_index("occ")
    role = (((index >> 1) ^ index) & 1) ^ 1
    kind = [(((i >> 1) ^ i) & 1) ^ 1 for i in range(peers)]

    def to_core(i):
        return i ^ 1

    def to_y(i):
        return i ^ 2

    def to_z(i):
        return (i + 4) % peers if (i >> 1) & 1 == 0 else (i - 4) % peers

    def send(value, where, only=None):
        pairs = [(i, where(i)) for i in range(peers) if only is None or kind[i] == only]
        return lax.ppermute(value, "occ", pairs)

    rows = vir // CHUNKS
    pieces = [lax.slice_in_dim(own, k * rows, (k + 1) * rows, axis=0) for k in range(CHUNKS)]
    first_y = [send(p, to_y, 1) for p in pieces]
    partner = send(own, to_core)
    partner_eps = send(occ_energy, to_core)
    chip_eps = jnp.concatenate([occ_energy, partner_eps])
    y_eps = send(chip_eps, to_y)
    z_eps = send(y_eps, to_z)
    is_e = role == 1
    eps = jnp.stack(
        [
            occ_energy[0],
            partner_eps[0],
            jnp.where(is_e, y_eps[1], y_eps[0]),
            jnp.where(is_e, z_eps[1], z_eps[0]),
            jnp.where(is_e, y_eps[0], y_eps[1]),
            jnp.where(is_e, z_eps[0], z_eps[1]),
        ]
    )
    role_v = role.astype(jnp.int32).reshape(1)
    vir_row = vir_energy.reshape(1, vir)
    run = functools.partial(stage, role=role_v, eps=eps, own=own, vir_row=vir_row)

    first_z = [send(p, to_z, 0) for p in first_y]
    first_d = [send(p, to_core, 0) for p in first_z]
    second_y = [send(tied(p, first_y[CHUNKS - 2]), to_y, 0) for p in pieces]
    second_z = [send(p, to_z, 1) for p in second_y]
    second_d = [send(p, to_core, 1) for p in second_y]

    every = tuple(range(CHUNKS))
    both = tuple(range(CHUNKS, 2 * CHUNKS))
    carry = run(
        "stage_a",
        [(0, ("own", "own"), ((1, 0), (1, 0))), (1, ((0,), (0,)), ((0, 0), (1, 1)))],
        [partner],
        None,
        False,
    )
    carry = run("stage_c", [(2, (every, None), ((1, 1), (0, 0)))], first_y, carry, False)
    carry = run("stage_d", [(3, (every, both), ((1, 1), (1, 0)))], first_z + first_d, carry, False)
    carry = run("stage_e", [(4, (every, both), ((1, 0), (0, 0)))], second_d + second_y, carry, False)
    density, _ = run("stage_f", [(5, (None, every), ((0, 0), (0, 0)))], second_z, carry, True)

    left = carry[1]
    bits = peers.bit_length() - 1
    left = left.reshape((2,) * bits + (vir // peers, vir))
    for bit in range(bits):
        axis = bits - 1 - bit
        mine = (index >> bit) & 1
        keep = lax.dynamic_index_in_dim(left, mine, axis, keepdims=False)
        give = lax.dynamic_index_in_dim(left, 1 - mine, axis, keepdims=False).astype(BF16)
        got = send(give, lambda i, bit=bit: i ^ (1 << bit))
        left = keep + got.astype(F32)
    factor = 2.0 / (peers * (2 * REACH + 1))
    return density[None], left * factor


def solution(mesh):
    peers = mesh.shape["occ"]
    assert peers >= 8 and peers & (peers - 1) == 0
    placed = (P(("geom", "occ"), None, None), P(("geom", "occ")), P("geom"))
    return jax.shard_map(
        per_device,
        mesh=mesh,
        in_specs=placed,
        out_specs=(P(("geom", "occ"), None, None), P(("geom", "occ"), None)),
        check_vma=False,
    )
```
